256 devices in a mesh: exp: 32 (over z, x), tp: 8 (over y, core).
Axes of the slice: x: 4, y: 4, z: 8, core: 2. Of those that a mesh axis runs over, the one named last changes fastest.
Arguments:
- tokens: bfloat16 [8192, 3584], P('exp', 'tp'), may hold values from -6 to 6
- cotangent: bfloat16 [8192, 3584], P('exp', 'tp'), may hold values from -3 to 3
- up_weight: bfloat16 [32, 3584, 2432], P('exp', None, 'tp'), may hold values from -0.09375 to 0.09375
- down_weight: bfloat16 [32, 2432, 3584], P('exp', 'tp'), may hold values from -0.125 to 0.125
- expert_ids: int32 [8192, 2], P('exp'), may hold values from 0 to 31, all different within a row; in each aligned block of 256 rows (0 to 255, 256 to 511, ...) at most 32 rows name the same one
- gate_probs: bfloat16 [8192, 2], P('exp'), may hold values from 0.049804688 to 0.94921875
Outputs:
- token_grad: bfloat16 [8192, 3584], P('exp', 'tp')
- up_grad: bfloat16 [32, 3584, 2432], P('exp', None, 'tp')
- down_grad: bfloat16 [32, 2432, 3584], P('exp', 'tp')
The draws below stay inside these ranges and needn't reach their ends.
Inputs may be any that keep to these rules, and one draw needn't show every extreme that they name: `expert_ids`: each row names 2 different experts. Among the 256 rows of one index of exp no expert is named more than 32 times, a bound that some block reaches.
All inputs are finite; a program needn't handle non-finite values.
Results may differ from the reference program's by a relative error of at most 0.019.
Values may be sent and summed in bfloat16 or wider, within the bound.
A program may use at most 128 MiB of HBM per device.

```python
import math
import jax
import jax.numpy as jnp
import numpy as np
from jax import lax

D = 3584
FF = 2432
TOP = 2
TOK_DEV = 256
EXPERTS = 32
TOKENS = 8192
SLOT = 32
CAP = 640
N_TP = 8


def block_levels(rng, shape, pieces, smallest, largest):
    gain = 1.0
    for dim, shards_of in pieces:
        steps = jax.random.uniform(jax.random.fold_in(jax.random.fold_in(rng, 6), dim), (shards_of,), jnp.float32, smallest / len(pieces), largest / len(pieces))
        gain = gain * jnp.repeat(jnp.exp(steps), shape[dim] // shards_of).reshape((-1,) + (1,) * (len(shape) - 1 - dim))
    return gain


def shared_out(rng, own, number, rows, count, top, reach, skew):
    ranking = jax.random.permutation(rng, count)
    crowded, common = shares(count, rows * top, reach, skew, True), shares(count, rows * top, reach, skew, False)
    places = jnp.arange(count)

    def named(lengths, turn):
        used = int((lengths > 0).sum())
        fixed = max(1, used // 4)
        moved = fixed + (places - fixed + turn * (used - fixed)) % max(1, count - fixed)
        return jnp.zeros((count,), jnp.int32).at[ranking[jnp.where(places < fixed, places, moved)]].set(jnp.asarray(lengths, jnp.int32))

    lengths = jnp.where(number % 4 == 0, named(crowded, number // 4), named(common, number - number // 4 - 1))
    mixed = jax.random.permutation(jax.random.fold_in(own, 3), count)
    giver, receiver = mixed[0:count // 2 * 2:2], mixed[1:count // 2 * 2:2]
    room = jnp.minimum(lengths[giver] - 1, reach - lengths[receiver]) // 2
    room = jnp.where((giver == ranking[0]) | (receiver == ranking[0]) | (lengths[receiver] == 0), 0, jnp.maximum(room, 0))
    moved = jax.random.randint(jax.random.fold_in(own, 4), (count // 2,), 0, 1 << 20) % (room + 1)
    lengths = lengths.at[giver].add(-moved).at[receiver].add(moved)
    items = jnp.searchsorted(jnp.cumsum(lengths), jnp.arange(rows * top), side="right").astype(jnp.int32)
    grid = items.reshape(top, rows).T
    grid = grid[jax.random.permutation(jax.random.fold_in(own, 1), rows)]
    turn = jax.random.randint(jax.random.fold_in(own, 2), (rows, 1), 0, top)
    return jnp.take_along_axis(grid, (jnp.arange(top)[None, :] + turn) % top, axis=1)


def shares(number_of, total, most, skew, full):
    loads = [(1 << 20) // math.isqrt(rank ** skew) + 1 for rank in range(1, number_of + 1)]
    largest = most if full else min(most, max(-(-total // number_of), total * loads[0] // sum(loads)))
    least = 1 if total - largest >= number_of - 1 else 0
    given, rest = [largest] + [least] * (number_of - 1), total - largest - least * (number_of - 1)
    while rest > 0:
        candidates = [i for i in range(1, number_of) if given[i] < largest] or [i for i in range(1, number_of) if given[i] < most]
        whole, left = sum([loads[i] for i in candidates]), rest
        for i in candidates:
            addition = min(most - given[i], max(1, left * loads[i] // whole), rest)
            given[i] = given[i] + addition
            rest = rest - addition
    return np.array(given)


def gaussian(rng, dims, width, bound, pieces=(), kind=jnp.bfloat16):
    values = width * jax.random.normal(rng, dims, jnp.float32)
    if pieces:
        values = values * block_levels(rng, dims, pieces, -0.22, 0.18)
    return jnp.clip(values, -bound, bound).astype(kind)


def setup_inputs(seed: int = 0) -> dict:
    arg_keys = jax.random.split(jax.random.key(seed), 7)
    tokens = gaussian(arg_keys[0], (TOKENS, D), 1.0, 6.0, ((0, 32), (1, 8)))
    cotangent = gaussian(arg_keys[1], (TOKENS, D), 0.5, 3.0, ((0, 32), (1, 8)))
    up_weight = gaussian(arg_keys[2], (EXPERTS, D, FF), D ** -0.5, 0.09375, ((0, 32), (2, 8)))
    down_weight = gaussian(arg_keys[3], (EXPERTS, FF, D), FF ** -0.5, 0.125, ((0, 32), (1, 8)))
    expert_ids_keys = jax.random.split(jax.random.fold_in(arg_keys[4], 1), TOKENS // TOK_DEV)
    expert_ids_turns = jax.random.permutation(jax.random.fold_in(arg_keys[4], 3), TOKENS // TOK_DEV)
    expert_ids = jax.vmap(lambda own, number: shared_out(jax.random.fold_in(arg_keys[4], 2), own, number, TOK_DEV, EXPERTS, TOP, SLOT, 2))(expert_ids_keys, expert_ids_turns).reshape((TOKENS, TOP))
    gate_probs = jnp.clip(0.049804688 + 0.89941406 * jax.random.uniform(arg_keys[5], (TOKENS, TOP), jnp.float32) ** block_levels(arg_keys[5], (TOKENS, TOP), ((0, 32),), -0.2, 0.2), 0.049804688, 0.94921875).astype(jnp.bfloat16)
    return dict(tokens=tokens, cotangent=cotangent, up_weight=up_weight, down_weight=down_weight, expert_ids=expert_ids, gate_probs=gate_probs)


def silu_parts(hidden):
    sigma = jax.nn.sigmoid(hidden)
    return hidden * sigma, sigma * (1.0 + hidden * (1.0 - sigma))


def reference(tokens, cotangent, up_weight, down_weight, expert_ids, gate_probs):
    flat_ids = expert_ids.reshape(-1).astype(jnp.int32)
    pairs = flat_ids.shape[0]
    onehot = (flat_ids[:, None] == jnp.arange(EXPERTS, dtype=jnp.int32)[None, :]).astype(jnp.int32)
    ranks = jnp.sum(onehot * (jnp.cumsum(onehot, axis=0) - 1), axis=1).astype(jnp.int32)
    keep = ranks < CAP
    target = jnp.where(keep, flat_ids * CAP + ranks, EXPERTS * CAP).astype(jnp.int32)
    source = jnp.zeros((EXPERTS * CAP + 1,), jnp.int32).at[target].set(jnp.arange(pairs, dtype=jnp.int32))
    filled = jnp.zeros((EXPERTS * CAP + 1,), jnp.int32).at[target].set(1)
    source = source[:-1].reshape(EXPERTS, CAP)
    filled = filled[:-1].reshape(EXPERTS, CAP)
    flat_probs = gate_probs.reshape(-1)
    block = FF // N_TP

    def one_expert(operands):
        rows, live, w_up, w_down = operands
        token_rows = (rows // TOP).astype(jnp.int32)
        alive = live > 0
        inputs = jnp.where(alive[:, None], tokens[token_rows], jnp.zeros_like(tokens[:1]))
        weights = jnp.where(alive, flat_probs[rows].astype(jnp.float32), jnp.float32(0.0))
        routed = (weights[:, None] * cotangent[token_rows].astype(jnp.float32)).astype(jnp.bfloat16)
        hidden = jnp.dot(inputs, w_up, preferred_element_type=jnp.float32)
        act_full, slope = silu_parts(hidden)
        act = act_full.astype(jnp.bfloat16)
        d_act = lax.dot_general(routed, w_down, (((1,), (1,)), ((), ())), preferred_element_type=jnp.float32)
        d_hidden = (d_act * slope).astype(jnp.bfloat16)
        grad_up = lax.dot_general(inputs, d_hidden, (((0,), (0,)), ((), ())), preferred_element_type=jnp.float32).astype(jnp.bfloat16)
        grad_down = lax.dot_general(act, routed, (((0,), (0,)), ((), ())), preferred_element_type=jnp.float32).astype(jnp.bfloat16)
        total = jnp.zeros((CAP, D), jnp.float32)
        for part in range(N_TP):
            piece = lax.dot_general(d_hidden[:, part * block:(part + 1) * block], w_up[:, part * block:(part + 1) * block], (((1,), (1,)), ((), ())), preferred_element_type=jnp.float32)
            rounded = lax.optimization_barrier(piece.astype(jnp.bfloat16))
            total = total + rounded.astype(jnp.float32)
        return grad_up, grad_down, total

    grads_up, grads_down, totals = lax.map(one_expert, (source, filled, up_weight, down_weight))
    flat_totals = jnp.concatenate([totals.reshape(EXPERTS * CAP, D), jnp.zeros((1, D), jnp.float32)], axis=0)
    per_pair = flat_totals[target]
    token_grad = jnp.sum(per_pair.reshape(TOKENS, TOP, D), axis=1).astype(jnp.bfloat16)
    return token_grad, grads_up, grads_down
```

```python
import jax
import jax.numpy as jnp
from jax import lax
from jax.sharding import PartitionSpec as P

BF = jnp.bfloat16
F32 = jnp.float32


def dot(a, b, dims):
    return lax.dot_general(a, b, (dims, ((), ())), preferred_element_type=F32)


def per_device(tokens, cotangent, up_weight, down_weight, expert_ids, gate_probs):
    tok_count, width = tokens.shape
    n_exp = lax.axis_size("exp")
    n_tp = lax.axis_size("tp")
    experts = n_exp
    slot = 4 * tok_count // experts
    cap = 5 * tok_count * n_exp // (2 * experts)
    rows = experts * slot
    hot = expert_ids[:, :, None] == jnp.arange(experts, dtype=jnp.int32)[None, None, :]
    named = jnp.any(hot, axis=1)
    weight = jnp.sum(jnp.where(hot, gate_probs[:, :, None].astype(F32), 0.0), axis=1)
    order = jnp.arange(tok_count)
    before = (order[None, :] < order[:, None]).astype(BF)
    rank = dot(before, named.astype(BF), ((1,), (0,))).astype(jnp.int32)
    sel = named[:, :, None] & (
        rank[:, :, None] == jnp.arange(slot, dtype=jnp.int32)[None, None, :]
    )
    pick = sel.reshape(tok_count, rows).astype(BF)
    pick_w = jnp.where(sel, weight[:, :, None], 0.0).reshape(tok_count, rows).astype(BF)
    send_x = dot(pick, tokens, ((0,), (0,))).astype(BF)
    send_r = dot(pick_w, cotangent, ((0,), (0,))).astype(BF)
    filled = dot(pick, jnp.ones((tok_count, 128), BF), ((0,), (0,))).astype(BF)
    send = jnp.concatenate([send_x, send_r, filled], axis=1)
    got = lax.all_to_all(send, "exp", split_axis=0, concat_axis=0, tiled=True)
    valid = got[:, 2 * width].astype(F32)
    slots = jnp.arange(rows)
    earlier = (slots[None, :] < slots[:, None]).astype(BF)
    place = dot(earlier, valid[:, None].astype(BF), ((1,), (0,)))[:, 0].astype(jnp.int32)
    place = jnp.where(valid > 0, place, rows)
    pack = (jnp.arange(cap)[:, None] == place[None, :]).astype(BF)
    packed = dot(pack, got[:, : 2 * width], ((1,), (0,))).astype(BF)
    full = lax.all_gather(packed, "tp", axis=0, tiled=False)
    w_up = up_weight[0]
    w_down = down_weight[0]
    x = jnp.moveaxis(full[:, :, :width], 0, 1).reshape(cap, n_tp * width)
    r = jnp.moveaxis(full[:, :, width:], 0, 1).reshape(cap, n_tp * width)
    hidden = dot(x, w_up, ((1,), (0,)))
    sigma = jax.nn.sigmoid(hidden)
    act = (hidden * sigma).astype(BF)
    d_act = dot(r, w_down, ((1,), (1,)))
    d_hidden = (d_act * (sigma * (1.0 + hidden * (1.0 - sigma)))).astype(BF)
    term = dot(d_hidden, w_up, ((1,), (1,))).astype(BF)
    summed = lax.psum_scatter(term, "tp", scatter_dimension=1, tiled=True)
    up_grad = dot(x, d_hidden, ((0,), (0,))).astype(BF)
    down_grad = dot(act, r, ((0,), (0,))).astype(BF)
    unpacked = dot(pack, summed.astype(BF), ((0,), (0,))).astype(BF)
    back = lax.all_to_all(unpacked, "exp", split_axis=0, concat_axis=0, tiled=True)
    token_grad = dot(pick, back, ((1,), (0,))).astype(BF)
    return (token_grad, up_grad[None], down_grad[None])


def solution(mesh):
    placed = (
        P("exp", "tp"),
        P("exp", "tp"),
        P("exp", None, "tp"),
        P("exp", "tp", None),
        P("exp", None),
        P("exp", None),
    )
    return jax.shard_map(
        per_device,
        mesh=mesh,
        in_specs=placed,
        out_specs=(P("exp", "tp"), P("exp", None, "tp"), P("exp", "tp", None)),
        check_vma=False,
    )
```

```python
import functools

import jax
import jax.numpy as jnp
from jax import lax
from jax.experimental import pallas as pl
from jax.experimental.pallas import tpu as pltpu
from jax.sharding import PartitionSpec as P

BF = jnp.bfloat16
F32 = jnp.float32
MESH = pl.DeviceIdType.MESH
FAR = 1e6


def dot(a, b, dims):
    return lax.dot_general(a, b, (dims, ((), ())), preferred_element_type=F32)


def iota(shape, dim):
    return lax.broadcasted_iota(jnp.int32, shape, dim).astype(F32)


def kernel(
    cfg,
    ids_ref, prob_ref, tok_ref, cot_ref, up_ref, down_ref,
    tg_ref, ug_ref, dg_ref,
    src, rk, ws, cnt, pick, pickw, send, recv, msend, mrecv, place, prow, pack, unpack,
    gath, wup, wdn, hid, dac, dh, dht, actt, part, sibr, pair, half, side, fin,
    rsend, rrecv, tgs, ugs, dgs,
    load_sem, swap_sem, meta_sem, a2a_sem, ag_s, ag_r, rs_s, rs_r, ret_sem,
):
    n_exp, n_tp, slot, cap, tok, width, ff, ffp, chunks, parts = cfg
    chip = 2 * width
    win = parts[-1][0] + parts[-1][1]
    rows = n_exp * slot
    mid = cap // 2
    ny = n_tp // 2
    me = lax.axis_index("exp")
    tp = lax.axis_index("tp")
    y = tp // 2
    core = tp % 2
    sib = tp + 1 - 2 * core
    y_right, y_left, y_opp = (y + 1) % ny, (y + ny - 1) % ny, (y + 2) % ny
    right, left = 2 * y_right + core, 2 * y_left + core

    def lanes(start, size):
        return pl.ds(pl.multiple_of(start, 128), size)

    def remote(a, b, s, r, device):
        return pltpu.make_async_remote_copy(
            src_ref=a, dst_ref=b, send_sem=s, recv_sem=r, device_id=device, device_id_type=MESH
        )

    def peers(fn):
        def step(d, carry):
            fn((me + d) % n_exp)
            return carry

        lax.fori_loop(1, n_exp, step, 0)

    load_up = pltpu.make_async_copy(up_ref, wup.at[pl.ds(0, ff), :], load_sem.at[0])
    load_dn = pltpu.make_async_copy(down_ref, wdn.at[pl.ds(0, ff), :], load_sem.at[1])
    load_tok = pltpu.make_async_copy(tok_ref, src.at[pl.ds(0, width), :], load_sem.at[2])
    load_cot = pltpu.make_async_copy(cot_ref, src.at[pl.ds(width, width), :], load_sem.at[2])

    barrier = pltpu.get_barrier_semaphore()
    peers(lambda d: pl.semaphore_signal(barrier, inc=1, device_id=(d, tp), device_id_type=MESH))
    for other in (sib, left, right):
        pl.semaphore_signal(barrier, inc=1, device_id=(me, other), device_id_type=MESH)

    @pl.when(core == 0)
    def _():
        load_tok.start()

    @pl.when(core == 1)
    def _():
        load_cot.start()

    load_up.start()
    load_dn.start()
    pl.semaphore_wait(barrier, n_exp - 1 + 3)

    swap_cot = remote(
        cot_ref, src.at[pl.ds(0, width), :], swap_sem.at[0], swap_sem.at[1], (me, sib)
    )
    swap_tok = remote(
        tok_ref, src.at[pl.ds(width, width), :], swap_sem.at[0], swap_sem.at[1], (me, sib)
    )

    @pl.when(core == 0)
    def _():
        swap_cot.start()

    @pl.when(core == 1)
    def _():
        swap_tok.start()

    expert = lax.broadcasted_iota(jnp.int32, (n_exp, tok), 0)
    hot0 = expert == ids_ref[0:1, :]
    hot1 = expert == ids_ref[1:2, :]
    probs = prob_ref[...].astype(F32)
    weight = jnp.where(hot0, probs[0:1, :], 0.0) + jnp.where(hot1, probs[1:2, :], 0.0)
    named = jnp.where(hot0, 1.0, 0.0) + jnp.where(hot1, 1.0, 0.0)
    earlier = jnp.where(
        lax.broadcasted_iota(jnp.int32, (tok, tok), 0)
        < lax.broadcasted_iota(jnp.int32, (tok, tok), 1),
        1.0,
        0.0,
    ).astype(BF)
    rank = dot(named.astype(BF), earlier, ((1,), (0,)))
    rk[...] = jnp.where(named > 0.0, rank, -1.0)
    ws[...] = jnp.where(core == 0, named, weight)
    cnt[...] = dot(named.astype(BF), jnp.ones((tok, 128), BF), ((1,), (0,)))

    def count_tile(e, carry):
        msend[e] = jnp.broadcast_to(cnt[pl.ds(e, 1), :], (8, 128))
        return carry

    lax.fori_loop(0, n_exp, count_tile, 0)
    peers(
        lambda d: remote(
            msend.at[d], mrecv.at[me], meta_sem.at[0], meta_sem.at[1], (d, tp)
        ).start()
    )
    mrecv[me] = msend[me]

    def build_pick(e, carry):
        at = pl.ds(pl.multiple_of(e * slot, slot), slot)
        hit = jnp.broadcast_to(rk[pl.ds(e, 1), :], (slot, tok)) == iota((slot, tok), 0)
        pick[at, :] = jnp.where(hit, 1.0, 0.0).astype(BF)
        pickw[at, :] = jnp.where(
            hit, jnp.broadcast_to(ws[pl.ds(e, 1), :], (slot, tok)), 0.0
        ).astype(BF)
        return carry

    lax.fori_loop(0, n_exp, build_pick, 0)

    def exchange(buf_from, buf_to, sems, c, c0, cw):
        mine = pl.ds(pl.multiple_of(me * slot, slot), slot)
        peers(
            lambda d: remote(
                buf_from.at[pl.ds(pl.multiple_of(d * slot, slot), slot), pl.ds(c0, cw)],
                buf_to.at[mine, pl.ds(c0, cw)],
                sems.at[c, 0],
                sems.at[c, 1],
                (d, tp),
            ).start()
        )
        buf_to[mine, c0 : c0 + cw] = buf_from[mine, c0 : c0 + cw]

    def exchanged(buf, sems, c, c0, cw, which):
        whole = buf.at[pl.ds(0, (n_exp - 1) * slot), pl.ds(c0, cw)]
        pltpu.make_async_copy(whole, whole, sems.at[c, which]).wait()

    load_tok.wait()
    swap_cot.wait_recv()
    block = min(rows, 256)
    for c, (c0, cw) in enumerate(chunks):

        def gather_rows(i, carry):
            at = pl.ds(pl.multiple_of(i * block, block), block)
            send[at, c0 : c0 + cw] = dot(
                pickw[at, :], src[c0 : c0 + cw, :], ((1,), (1,))
            ).astype(BF)
            return carry

        lax.fori_loop(0, rows // block, gather_rows, 0)
        exchange(send, recv, a2a_sem, c, c0, cw)

    wait_meta = mrecv.at[pl.ds(0, n_exp - 1)]
    pltpu.make_async_copy(wait_meta, wait_meta, meta_sem.at[1]).wait()

    def place_rows(g, before):
        at = pl.ds(pl.multiple_of(g * slot, slot), slot)
        number = iota((slot, 128), 0)
        count = mrecv[g]
        place[at, :] = jnp.where(
            number < jnp.broadcast_to(count[0:1, :], (slot, 128)),
            jnp.broadcast_to(before[0:1, :], (slot, 128)) + number,
            FAR,
        )
        return before + count

    lax.fori_loop(0, n_exp, place_rows, jnp.zeros((8, 128), F32))
    prow[...] = jnp.transpose(place[...])[0:8, :]

    def build_pack(i, carry):
        at = pl.ds(pl.multiple_of(i * 64, 64), 64)
        row = jnp.broadcast_to(prow[0:1, :], (64, rows))
        pack[at, :] = jnp.where(
            row == iota((64, rows), 0) + (i * 64).astype(F32), 1.0, 0.0
        ).astype(BF)
        return carry

    lax.fori_loop(0, cap // 64, build_pack, 0)
    wup[pl.ds(ff, ffp - ff), :] = jnp.zeros((ffp - ff, ny * chip), BF)
    wdn[pl.ds(ff, ffp - ff), :] = jnp.zeros((ffp - ff, ny * chip), BF)

    def cols(yy, c):
        return lanes(yy * chip + chunks[c][0], chunks[c][1])

    top, low, full = pl.ds(0, mid), pl.ds(mid, mid), pl.ds(0, cap)

    def ag(k, c, receive):
        if k == 0:
            where, span, device = (y_left if receive else y), full, right
        elif k == 1:
            where, span, device = (y_right if receive else y), full, left
        elif k == 2:
            where, span, device = y, full, sib
        elif k == 3:
            where, span, device = y_left, full, sib
        elif k == 4:
            where, span, device = y_right, full, sib
        elif k == 5:
            where, span, device = (y_opp if receive else y_left), top, right
        elif k == 6:
            where, span, device = (y_opp if receive else y_right), low, left
        elif k == 7:
            where, span, device = y_opp, top, sib
        else:
            where, span, device = y_opp, low, sib
        plane = (1 - core) if (receive and k in (2, 3, 4, 7, 8)) else core
        at = gath.at[plane, span, cols(where, c)]
        return remote(at, at, ag_s.at[c, k], ag_r.at[c, k], (me, device))

    def forward_near(c):
        ag(0, c, True).wait_recv()
        ag(5, c, False).start()
        ag(3, c, False).start()
        ag(1, c, True).wait_recv()
        ag(6, c, False).start()
        ag(4, c, False).start()

    def forward_far(c):
        ag(5, c, True).wait_recv()
        ag(7, c, False).start()
        ag(6, c, True).wait_recv()
        ag(8, c, False).start()

    last = len(chunks) - 1
    for c, (c0, cw) in enumerate(chunks):
        exchanged(recv, a2a_sem, c, c0, cw, 1)
        gath[core, :, cols(y, c)] = dot(
            pack[...], recv[:, c0 : c0 + cw], ((1,), (0,))
        ).astype(BF)
        for k in (0, 1, 2):
            ag(k, c, False).start()
        if c >= 1:
            forward_near(c - 1)
        if c >= 2:
            forward_far(c - 2)

    load_up.wait()
    load_dn.wait()
    hid[...] = jnp.zeros_like(hid)
    dac[...] = jnp.zeros_like(dac)

    def accumulate(yy):
        at = lanes(yy * chip, chip)
        hid[...] += dot(gath[0, :, at], wup[:, at], ((1,), (1,)))
        dac[...] += dot(gath[1, :, at], wdn[:, at], ((1,), (1,)))

    def arrived(*kinds):
        for c in range(len(chunks)):
            for k in kinds:
                ag(k, c, True).wait_recv()

    forward_near(last)
    if last >= 1:
        forward_far(last - 1)
    arrived(2)
    accumulate(y)
    forward_far(last)

    def build_unpack(g, carry):
        at = pl.ds(pl.multiple_of(g * slot, slot), slot)
        for b in range(cap // 128):
            unpack[at, 128 * b : 128 * b + 128] = jnp.where(
                place[at, :] == iota((slot, 128), 1) + 128.0 * b, 1.0, 0.0
            ).astype(BF)
        return carry

    lax.fori_loop(0, n_exp, build_unpack, 0)
    arrived(3)
    accumulate(y_left)
    arrived(4)
    accumulate(y_right)
    arrived(7, 8)
    accumulate(y_opp)

    rb = 64

    def activate(i, carry):
        at = pl.ds(pl.multiple_of(i * rb, rb), rb)
        h = hid[at, :]
        s = jax.nn.sigmoid(h)
        dac[at, :] = dac[at, :] * (s * (1.0 + h * (1.0 - s)))
        hid[at, :] = h * s
        dh[at, :] = dac[at, :].astype(BF)
        return carry

    lax.fori_loop(0, cap // rb, activate, 0)

    dests = (y_opp, y_right, y_left, y)
    my_win, sib_win = (chip - win) * core, (chip - win) * (1 - core)

    def to_sib(k):
        return remote(
            part.at[k, :, lanes(sib_win, win)], sibr.at[k], rs_s.at[0, k], rs_r.at[0, k], (me, sib)
        )

    for k, yy in enumerate(dests):
        part[k] = dot(dh[...], wup[:, lanes(yy * chip, chip)], ((1,), (0,))).astype(BF)
        to_sib(k).start()
    dht[...] = jnp.transpose(dac[...]).astype(BF)
    actt[...] = jnp.transpose(hid[...]).astype(BF)

    def both(k):
        mine = part[k, :, lanes(my_win, win)].astype(F32)
        return mine + sibr[k].astype(F32)

    def far(h, k):
        p0, pw = parts[h]
        return remote(
            pair.at[0, (top, low)[k], pl.ds(p0, pw)],
            half.at[k, :, pl.ds(p0, pw)],
            rs_s.at[1 + h, k],
            rs_r.at[1 + h, k],
            (me, (right, left)[k]),
        )

    def near(h, k):
        p0, pw = parts[h]
        return remote(
            pair.at[1 + k, :, pl.ds(p0, pw)],
            side.at[k, :, pl.ds(p0, pw)],
            rs_s.at[1 + h, 2 + k],
            rs_r.at[1 + h, 2 + k],
            (me, (right, left)[k]),
        )

    to_sib(0).wait_recv()
    pair[0] = both(0).astype(BF)
    for h in range(len(parts)):
        far(h, 0).start()
        far(h, 1).start()
    to_sib(1).wait_recv()
    pair[1] = both(1).astype(BF)
    to_sib(2).wait_recv()
    pair[2] = both(2).astype(BF)

    gb = 512 if (ny * chip) % 512 == 0 else 128

    def grad_up(i, carry):
        at = lanes(i * gb, gb)
        ugs[:, at] = dot(dht[...], gath[0, :, at], ((1,), (0,)))[:ff].astype(BF)
        return carry

    def grad_down(i, carry):
        at = lanes(i * gb, gb)
        dgs[:, at] = dot(actt[...], gath[1, :, at], ((1,), (0,)))[:ff].astype(BF)
        return carry

    store_up = pltpu.make_async_copy(ugs, ug_ref, load_sem.at[3])
    store_dn = pltpu.make_async_copy(dgs, dg_ref, load_sem.at[4])
    for h, (p0, pw) in enumerate(parts):
        for k in range(2):
            far(h, k).wait_recv()
            span = (top, low)[k]
            pair[1 + k, span, p0 : p0 + pw] = (
                pair[1 + k, span, p0 : p0 + pw].astype(F32) + half[k, :, p0 : p0 + pw].astype(F32)
            ).astype(BF)
            near(h, k).start()
    to_sib(3).wait_recv()
    lax.fori_loop(0, ny * chip // gb, grad_up, 0)
    store_up.start()
    for h, (p0, pw) in enumerate(parts):
        near(h, 0).wait_recv()
        near(h, 1).wait_recv()
        own = part[3, :, lanes(my_win + p0, pw)].astype(F32) + sibr[3, :, p0 : p0 + pw].astype(F32)
        fin[:, p0 : p0 + pw] = (
            own + side[0, :, p0 : p0 + pw].astype(F32) + side[1, :, p0 : p0 + pw].astype(F32)
        ).astype(BF)
        rsend[:, p0 : p0 + pw] = dot(unpack[...], fin[:, p0 : p0 + pw], ((1,), (0,))).astype(BF)
        exchange(rsend, rrecv, ret_sem, h, p0, pw)
    lax.fori_loop(0, ny * chip // gb, grad_down, 0)
    store_dn.start()

    for h, (p0, pw) in enumerate(parts):
        exchanged(rrecv, ret_sem, h, p0, pw, 1)
        tgs[p0 : p0 + pw, :] = dot(rrecv[:, p0 : p0 + pw], pick[...], ((0,), (0,))).astype(BF)
    result = pltpu.make_async_copy(
        tgs.at[pl.ds(pl.multiple_of((win - width) * core, 64), width), :], tg_ref, load_sem.at[2]
    )
    result.start()

    swap_cot.wait_send()
    wait_meta = msend.at[pl.ds(0, n_exp - 1)]
    pltpu.make_async_copy(wait_meta, wait_meta, meta_sem.at[0]).wait()
    for c, (c0, cw) in enumerate(chunks):
        exchanged(send, a2a_sem, c, c0, cw, 0)
        for k in range(9):
            ag(k, c, False).wait_send()
    for k in range(4):
        to_sib(k).wait_send()
    for h, (p0, pw) in enumerate(parts):
        for k in range(2):
            far(h, k).wait_send()
            near(h, k).wait_send()
        exchanged(rsend, ret_sem, h, p0, pw, 0)
    store_up.wait()
    store_dn.wait()
    result.wait()


def layer(cfg, ids, probs, tok_t, cot_t, up_t, down):
    n_exp, n_tp, slot, cap, tok, width, ff, ffp, chunks, parts = cfg
    chip = 2 * width
    wide = n_tp * width
    rows = n_exp * slot
    win = parts[-1][0] + parts[-1][1]
    n_c, n_p = len(chunks), len(parts)
    vm = pltpu.VMEM
    dma = pltpu.SemaphoreType.DMA
    hbm = pl.BlockSpec(memory_space=pl.ANY)
    vmem = pl.BlockSpec(memory_space=pltpu.VMEM)
    return pl.pallas_call(
        functools.partial(kernel, cfg),
        out_shape=(
            jax.ShapeDtypeStruct((width, tok), BF),
            jax.ShapeDtypeStruct((ff, wide), BF),
            jax.ShapeDtypeStruct((ff, wide), BF),
        ),
        in_specs=[vmem, vmem, hbm, hbm, hbm, hbm],
        out_specs=(hbm, hbm, hbm),
        scratch_shapes=[
            vm((chip, tok), BF), vm((n_exp, tok), F32), vm((n_exp, tok), F32), vm((n_exp, 128), F32),
            vm((rows, tok), BF), vm((rows, tok), BF), vm((rows, chip), BF), vm((rows, chip), BF),
            vm((n_exp, 8, 128), F32), vm((n_exp, 8, 128), F32), vm((rows, 128), F32), vm((8, rows), F32),
            vm((cap, rows), BF), vm((rows, cap), BF),
            vm((2, cap, wide), BF), vm((ffp, wide), BF), vm((ffp, wide), BF),
            vm((cap, ffp), F32), vm((cap, ffp), F32), vm((cap, ffp), BF), vm((ffp, cap), BF), vm((ffp, cap), BF),
            vm((4, cap, chip), BF), vm((4, cap, win), BF), vm((3, cap, win), BF),
            vm((2, cap // 2, win), BF), vm((2, cap, win), BF), vm((cap, win), BF),
            vm((rows, win), BF), vm((rows, win), BF), vm((win, tok), BF), vm((ff, wide), BF), vm((ff, wide), BF),
            dma((5,)), dma((2,)), dma((2,)), dma((n_c, 2)), dma((n_c, 9)), dma((n_c, 9)),
            dma((1 + n_p, 4)), dma((1 + n_p, 4)), dma((n_p, 2)),
        ],
        compiler_params=pltpu.CompilerParams(
            collective_id=0, has_side_effects=True, vmem_limit_bytes=60 << 20
        ),
    )(ids, probs, tok_t, cot_t, up_t, down)


def per_device(tokens, cotangent, up_weight, down_weight, expert_ids, gate_probs):
    tok, width = tokens.shape
    ff = up_weight.shape[2]
    n_exp = lax.axis_size("exp")
    n_tp = lax.axis_size("tp")
    slot = 4 * tok // n_exp
    cap = 5 * tok * n_exp // (2 * n_exp)
    ffp = -(-ff // 128) * 128
    chunks = ((0, 256), (256, 256), (512, 256), (768, 128))
    parts = ((0, 256), (256, 256))
    cfg = (n_exp, n_tp, slot, cap, tok, width, ff, ffp, chunks, parts)
    tg, ug, dg = layer(
        cfg, expert_ids.T, gate_probs.T, tokens.T, cotangent.T, up_weight[0].T, down_weight[0]
    )
    return (tg.T, ug.T[None], dg[None])


def solution(mesh):
    placed = (
        P("exp", "tp"),
        P("exp", "tp"),
        P("exp", None, "tp"),
        P("exp", "tp", None),
        P("exp", None),
        P("exp", None),
    )
    return jax.shard_map(
        per_device,
        mesh=mesh,
        in_specs=placed,
        out_specs=(P("exp", "tp"), P("exp", None, "tp"), P("exp", "tp", None)),
        check_vma=False,
    )
```

```python
import functools

import jax
import jax.numpy as jnp
from jax import lax
from jax.experimental import pallas as pl
from jax.experimental.pallas import tpu as pltpu
from jax.sharding import PartitionSpec as P

BF = jnp.bfloat16
F32 = jnp.float32
MESH = pl.DeviceIdType.MESH
FAR = 1e6
AHEAD = 2
VM = 60
CHUNKS = tuple((128 * i, 128) for i in range(7))
PARTS = tuple((128 * i, 128) for i in range(4))


def dot(a, b, dims):
    return lax.dot_general(a, b, (dims, ((), ())), preferred_element_type=F32)


def iota(shape, dim):
    return lax.broadcasted_iota(jnp.int32, shape, dim).astype(F32)


def kernel(
    cfg,
    ids_ref, prob_ref, tok_ref, cot_ref, up_ref, down_ref,
    tg_ref, ug_ref, dg_ref,
    src, rk, ws, cnt, pick, pickw, send, recv, msend, mrecv, place, prow, pack, unpack,
    gath, wup, wdn, hid, dac, dh, dht, actt, own, pair, half, side, fin,
    rsend, rrecv, tgs, ugs, dgs,
    enter_sem, load_sem, swap_sem, meta_sem, a2a_sem, ag_s, ag_r, rs_s, rs_r, ret_sem,
):
    n_exp, n_tp, slot, cap, tok, width, ff, ffp, chunks, parts = cfg
    n_x = 4 if n_exp % 4 == 0 else 2
    chip = 2 * width
    win = parts[-1][0] + parts[-1][1]
    rows = n_exp * slot
    mid = cap // 2
    ny = n_tp // 2
    me = lax.axis_index("exp")
    tp = lax.axis_index("tp")
    y = tp // 2
    core = tp % 2
    sib = tp + 1 - 2 * core
    y_right, y_left, y_opp = (y + 1) % ny, (y + ny - 1) % ny, (y + 2) % ny
    right, left = 2 * y_right + core, 2 * y_left + core

    def lanes(start, size):
        return pl.ds(pl.multiple_of(start, 128), size)

    def remote(a, b, s, r, device):
        return pltpu.make_async_remote_copy(
            src_ref=a, dst_ref=b, send_sem=s, recv_sem=r, device_id=device, device_id_type=MESH
        )

    def peers(fn):
        def step(d, carry):
            fn((me + d) % n_exp)
            return carry

        lax.fori_loop(1, n_exp, step, 0)

    load_up = pltpu.make_async_copy(up_ref, wup.at[pl.ds(0, ff), :], load_sem.at[0])
    load_dn = pltpu.make_async_copy(down_ref, wdn.at[pl.ds(0, ff), :], load_sem.at[1])
    load_tok = pltpu.make_async_copy(tok_ref, src.at[pl.ds(0, width), :], load_sem.at[2])
    load_cot = pltpu.make_async_copy(cot_ref, src.at[pl.ds(width, width), :], load_sem.at[2])

    barrier = pltpu.get_barrier_semaphore()

    def signal(sem, exp, other):
        pl.semaphore_signal(sem, inc=1, device_id=(exp, other), device_id_type=MESH)

    row = [me - me % n_x + (me + d) % n_x for d in range(1, n_x)]
    column = [(me + n_x * d) % n_exp for d in range(1, n_exp // n_x)]
    for d in row + column:
        signal(barrier, d, tp)
    for other in (sib, left, right):
        signal(barrier, me, other)

    @pl.when(core == 0)
    def _():
        load_tok.start()

    @pl.when(core == 1)
    def _():
        load_cot.start()

    load_up.start()
    load_dn.start()
    swap_up = remote(
        up_ref, wup.at[pl.ds(ffp, ff), :], swap_sem.at[2], swap_sem.at[3], (me, sib)
    )

    expert = lax.broadcasted_iota(jnp.int32, (n_exp, tok), 0)
    hot0 = expert == ids_ref[0:1, :]
    hot1 = expert == ids_ref[1:2, :]
    probs = prob_ref[...].astype(F32)
    weight = jnp.where(hot0, probs[0:1, :], 0.0) + jnp.where(hot1, probs[1:2, :], 0.0)
    named = jnp.where(hot0, 1.0, 0.0) + jnp.where(hot1, 1.0, 0.0)
    earlier = jnp.where(
        lax.broadcasted_iota(jnp.int32, (tok, tok), 0)
        < lax.broadcasted_iota(jnp.int32, (tok, tok), 1),
        1.0,
        0.0,
    ).astype(BF)
    rank = dot(named.astype(BF), earlier, ((1,), (0,)))
    rk[...] = jnp.where(named > 0.0, rank, -1.0)
    ws[...] = jnp.where(core == 0, named, weight)
    cnt[...] = dot(named.astype(BF), jnp.ones((tok, 128), BF), ((1,), (0,)))

    def count_tile(e, carry):
        msend[e] = jnp.broadcast_to(cnt[pl.ds(e, 1), :], (8, 128))
        return carry

    lax.fori_loop(0, n_exp, count_tile, 0)
    mrecv[me] = msend[me]

    pl.semaphore_wait(barrier, len(row) + len(column) + 3)
    for d in row:
        signal(enter_sem, d, tp)

    swap_cot = remote(
        cot_ref, src.at[pl.ds(0, width), :], swap_sem.at[0], swap_sem.at[1], (me, sib)
    )
    swap_tok = remote(
        tok_ref, src.at[pl.ds(width, width), :], swap_sem.at[0], swap_sem.at[1], (me, sib)
    )

    @pl.when(core == 0)
    def _():
        swap_cot.start()

    @pl.when(core == 1)
    def _():
        swap_tok.start()

    swap_up.start()

    def build_pick(e, carry):
        at = pl.ds(pl.multiple_of(e * slot, slot), slot)
        hit = jnp.broadcast_to(rk[pl.ds(e, 1), :], (slot, tok)) == iota((slot, tok), 0)
        pick[at, :] = jnp.where(hit, 1.0, 0.0).astype(BF)
        pickw[at, :] = jnp.where(
            hit, jnp.broadcast_to(ws[pl.ds(e, 1), :], (slot, tok)), 0.0
        ).astype(BF)
        return carry

    lax.fori_loop(0, n_exp, build_pick, 0)

    def first(c, plane):
        start, size = chunks[c]
        return pl.multiple_of(start + plane * (chip - size - 2 * start), 128)

    def exchange(buf_from, buf_to, sems, c, c0, cw):
        mine = pl.ds(pl.multiple_of(me * slot, slot), slot)
        peers(
            lambda d: remote(
                buf_from.at[pl.ds(pl.multiple_of(d * slot, slot), slot), pl.ds(c0, cw)],
                buf_to.at[mine, pl.ds(c0, cw)],
                sems.at[c, 0],
                sems.at[c, 1],
                (d, tp),
            ).start()
        )
        buf_to[mine, pl.ds(c0, cw)] = buf_from[mine, pl.ds(c0, cw)]

    def exchanged(buf, sems, c, c0, cw, which):
        whole = buf.at[pl.ds(0, (n_exp - 1) * slot), pl.ds(c0, cw)]
        pltpu.make_async_copy(whole, whole, sems.at[c, which]).wait()

    load_tok.wait()
    block = min(rows, 256)
    def send_chunk(c):
        c0, cw = first(c, core), chunks[c][1]

        def gather_rows(i, carry):
            at = pl.ds(pl.multiple_of(i * block, block), block)
            send[at, pl.ds(c0, cw)] = dot(
                pickw[at, :], src[pl.ds(c0, cw), :], ((1,), (1,))
            ).astype(BF)
            return carry

        lax.fori_loop(0, rows // block, gather_rows, 0)

    def start_chunk(c):
        exchange(send, recv, a2a_sem, c, first(c, core), chunks[c][1])

    send_chunk(0)
    pl.semaphore_wait(enter_sem, len(row))
    peers(
        lambda d: remote(
            msend.at[d], mrecv.at[me], meta_sem.at[0], meta_sem.at[1], (d, tp)
        ).start()
    )
    start_chunk(0)
    swap_cot.wait_recv()
    for c in range(1, min(AHEAD, len(chunks))):
        send_chunk(c)
        start_chunk(c)

    wait_meta = mrecv.at[pl.ds(0, n_exp - 1)]
    pltpu.make_async_copy(wait_meta, wait_meta, meta_sem.at[1]).wait()

    def place_rows(g, before):
        at = pl.ds(pl.multiple_of(g * slot, slot), slot)
        number = iota((slot, 128), 0)
        count = mrecv[g]
        place[at, :] = jnp.where(
            number < jnp.broadcast_to(count[0:1, :], (slot, 128)),
            jnp.broadcast_to(before[0:1, :], (slot, 128)) + number,
            FAR,
        )
        return before + count

    lax.fori_loop(0, n_exp, place_rows, jnp.zeros((8, 128), F32))
    prow[...] = jnp.transpose(place[...])[0:8, :]

    def build_pack(i, carry):
        at = pl.ds(pl.multiple_of(i * 64, 64), 64)
        row = jnp.broadcast_to(prow[0:1, :], (64, rows))
        pack[at, :] = jnp.where(
            row == iota((64, rows), 0) + (i * 64).astype(F32), 1.0, 0.0
        ).astype(BF)
        return carry

    lax.fori_loop(0, cap // 64, build_pack, 0)
    for at in (ff, ffp + ff):
        wup[pl.ds(at, ffp - ff), :] = jnp.zeros((ffp - ff, ny * chip), BF)
    wdn[pl.ds(ff, ffp - ff), :] = jnp.zeros((ffp - ff, ny * chip), BF)

    def cols(yy, c, plane):
        return lanes(yy * chip + first(c, plane), chunks[c][1])

    top, low, full = pl.ds(0, mid), pl.ds(mid, mid), pl.ds(0, cap)

    def ag(k, c, receive):
        if k == 0:
            where, span, device = (y_left if receive else y), full, right
        elif k == 1:
            where, span, device = (y_right if receive else y), full, left
        elif k == 2:
            where, span, device = y, full, sib
        elif k == 3:
            where, span, device = y_left, full, sib
        elif k == 4:
            where, span, device = y_right, full, sib
        elif k == 5:
            where, span, device = (y_opp if receive else y_left), top, right
        elif k == 6:
            where, span, device = (y_opp if receive else y_right), low, left
        elif k == 7:
            where, span, device = y_opp, top, sib
        else:
            where, span, device = y_opp, low, sib
        plane = (1 - core) if (receive and k in (2, 3, 4, 7, 8)) else core
        at = gath.at[plane, span, cols(where, c, plane)]
        return remote(at, at, ag_s.at[c, k], ag_r.at[c, k], (me, device))

    def forward_near(c):
        ag(0, c, True).wait_recv()
        ag(5, c, False).start()
        ag(3, c, False).start()
        ag(1, c, True).wait_recv()
        ag(6, c, False).start()
        ag(4, c, False).start()

    def forward_far(c):
        ag(5, c, True).wait_recv()
        ag(7, c, False).start()
        ag(6, c, True).wait_recv()
        ag(8, c, False).start()

    last = len(chunks) - 1
    for c, (c0, cw) in enumerate(chunks):
        if c + AHEAD < len(chunks):
            exchanged(send, a2a_sem, c, c0, cw, 0)
            send_chunk(c + AHEAD)
            start_chunk(c + AHEAD)
        exchanged(recv, a2a_sem, c, c0, cw, 1)
        gath[core, :, cols(y, c, core)] = dot(
            pack[...], recv[:, pl.ds(first(c, core), cw)], ((1,), (0,))
        ).astype(BF)
        for k in (0, 1, 2):
            ag(k, c, False).start()
        if c >= 1:
            forward_near(c - 1)
        if c >= 2:
            forward_far(c - 2)

    load_up.wait()
    load_dn.wait()
    hid[...] = jnp.zeros_like(hid)
    dac[...] = jnp.zeros_like(dac)

    def accumulate(yy):
        at = lanes(yy * chip, chip)
        hid[...] += dot(gath[0, :, at], wup[pl.ds(0, ffp), at], ((1,), (1,)))
        dac[...] += dot(gath[1, :, at], wdn[:, at], ((1,), (1,)))

    def arrived(*kinds):
        for c in range(len(chunks)):
            for k in kinds:
                ag(k, c, True).wait_recv()

    forward_near(last)
    if last >= 1:
        forward_far(last - 1)
    arrived(2)
    accumulate(y)
    forward_far(last)

    def build_unpack(g, carry):
        at = pl.ds(pl.multiple_of(g * slot, slot), slot)
        for b in range(cap // 128):
            unpack[at, 128 * b : 128 * b + 128] = jnp.where(
                place[at, :] == iota((slot, 128), 1) + 128.0 * b, 1.0, 0.0
            ).astype(BF)
        return carry

    lax.fori_loop(0, n_exp, build_unpack, 0)
    arrived(3)
    accumulate(y_left)
    arrived(4)
    accumulate(y_right)
    arrived(7, 8)
    accumulate(y_opp)

    rb = 64

    def activate(i, carry):
        at = pl.ds(pl.multiple_of(i * rb, rb), rb)
        h = hid[at, :]
        s = jax.nn.sigmoid(h)
        dac[at, :] = dac[at, :] * (s * (1.0 + h * (1.0 - s)))
        hid[at, :] = h * s
        dh[at, 0:ffp] = dac[at, :].astype(BF)
        return carry

    lax.fori_loop(0, cap // rb, activate, 0)

    dests = (y_opp, y_right, y_left, y)
    my_win = (chip - win) * core
    swap_dh = remote(
        dh.at[:, pl.ds(0, ffp)], dh.at[:, pl.ds(ffp, ffp)], swap_sem.at[4], swap_sem.at[5], (me, sib)
    )
    swap_dh.start()
    swap_up.wait_recv()
    swap_dh.wait_recv()

    def term(k):
        at = lanes(dests[k] * chip + my_win, win)
        return dot(dh[...], wup[:, at], ((1,), (0,)))

    ahead, behind = (top, low), (low, top)

    def step(h, kind, k):
        p0, pw = parts[h]
        at = pl.ds(p0, pw)
        span = behind[k] if kind == 1 else ahead[k]
        a = pair.at[0 if kind == 0 else 1 + k, span, at]
        b = half.at[k, :, at] if kind == 0 else side.at[k, span, at]
        n = 2 * kind + k
        return remote(a, b, rs_s.at[h, n], rs_r.at[h, n], (me, (right, left)[k]))

    def relay(h):
        p0, pw = parts[h]
        for k in range(2):
            step(h, 0, k).wait_recv()
            span = ahead[k]
            pair[1 + k, span, p0 : p0 + pw] = (
                pair[1 + k, span, p0 : p0 + pw].astype(F32) + half[k, :, p0 : p0 + pw].astype(F32)
            ).astype(BF)
            step(h, 2, k).start()

    def finish(h):
        p0, pw = parts[h]
        for kind in (1, 2):
            for k in range(2):
                step(h, kind, k).wait_recv()
        fin[:, p0 : p0 + pw] = (
            own[:, p0 : p0 + pw] + side[0, :, p0 : p0 + pw].astype(F32) + side[1, :, p0 : p0 + pw].astype(F32)
        ).astype(BF)
        rsend[:, p0 : p0 + pw] = dot(unpack[...], fin[:, p0 : p0 + pw], ((1,), (0,))).astype(BF)
        exchange(rsend, rrecv, ret_sem, h, p0, pw)

    gb = 512 if (ny * chip) % 512 == 0 else 128
    n_g = ny * chip // gb

    def grad_up(i, carry):
        at = lanes(i * gb, gb)
        ugs[:, at] = dot(dht[...], gath[0, :, at], ((1,), (0,)))[:ff].astype(BF)
        return carry

    def grad_down(i, carry):
        at = lanes(i * gb, gb)
        dgs[:, at] = dot(actt[...], gath[1, :, at], ((1,), (0,)))[:ff].astype(BF)
        return carry

    store_up = pltpu.make_async_copy(ugs, ug_ref, load_sem.at[3])
    store_dn = pltpu.make_async_copy(dgs, dg_ref, load_sem.at[4])
    n_h = len(parts)
    pair[0] = term(0).astype(BF)
    for k in range(2):
        step(0, 0, k).start()
    pair[1] = term(1).astype(BF)
    step(0, 1, 0).start()
    pair[2] = term(2).astype(BF)
    step(0, 1, 1).start()
    for k in range(2):
        step(1, 0, k).start()
    own[...] = term(3)
    dht[...] = jnp.transpose(dac[...]).astype(BF)
    for h in range(n_h):
        relay(h)
        for kind, q in ((1, h + 1), (0, h + 2)):
            if q < n_h:
                for k in range(2):
                    step(q, kind, k).start()
        if h > 0:
            finish(h - 1)
        lax.fori_loop(h * n_g // n_h, (h + 1) * n_g // n_h, grad_up, 0)
    store_up.start()
    finish(n_h - 1)
    actt[...] = jnp.transpose(hid[...]).astype(BF)
    lax.fori_loop(0, ny * chip // gb, grad_down, 0)
    store_dn.start()

    for h, (p0, pw) in enumerate(parts):
        exchanged(rrecv, ret_sem, h, p0, pw, 1)
        tgs[p0 : p0 + pw, :] = dot(rrecv[:, p0 : p0 + pw], pick[...], ((0,), (0,))).astype(BF)
    result = pltpu.make_async_copy(
        tgs.at[pl.ds(pl.multiple_of((win - width) * core, 64), width), :], tg_ref, load_sem.at[2]
    )
    result.start()

    swap_cot.wait_send()
    wait_meta = msend.at[pl.ds(0, n_exp - 1)]
    pltpu.make_async_copy(wait_meta, wait_meta, meta_sem.at[0]).wait()
    for c, (c0, cw) in enumerate(chunks):
        if c + AHEAD >= len(chunks):
            exchanged(send, a2a_sem, c, c0, cw, 0)
        for k in range(9):
            ag(k, c, False).wait_send()
    swap_up.wait_send()
    swap_dh.wait_send()
    for h, (p0, pw) in enumerate(parts):
        for kind in range(3):
            for k in range(2):
                step(h, kind, k).wait_send()
        exchanged(rsend, ret_sem, h, p0, pw, 0)
    store_up.wait()
    store_dn.wait()
    result.wait()


def layer(cfg, ids, probs, tok_t, cot_t, up_t, down):
    n_exp, n_tp, slot, cap, tok, width, ff, ffp, chunks, parts = cfg
    chip = 2 * width
    wide = n_tp * width
    rows = n_exp * slot
    win = parts[-1][0] + parts[-1][1]
    n_c, n_p = len(chunks), len(parts)
    vm = pltpu.VMEM
    dma = pltpu.SemaphoreType.DMA
    hbm = pl.BlockSpec(memory_space=pl.ANY)
    vmem = pl.BlockSpec(memory_space=pltpu.VMEM)
    return pl.pallas_call(
        functools.partial(kernel, cfg),
        out_shape=(
            jax.ShapeDtypeStruct((width, tok), BF),
            jax.ShapeDtypeStruct((ff, wide), BF),
            jax.ShapeDtypeStruct((ff, wide), BF),
        ),
        in_specs=[vmem, vmem] + [pl.BlockSpec(memory_space=pltpu.HBM)] * 4,
        out_specs=(hbm, hbm, hbm),
        scratch_shapes=[
            vm((chip, tok), BF), vm((n_exp, tok), F32), vm((n_exp, tok), F32), vm((n_exp, 128), F32),
            vm((rows, tok), BF), vm((rows, tok), BF), vm((rows, chip), BF), vm((rows, chip), BF),
            vm((n_exp, 8, 128), F32), vm((n_exp, 8, 128), F32), vm((rows, 128), F32), vm((8, rows), F32),
            vm((cap, rows), BF), vm((rows, cap), BF),
            vm((2, cap, wide), BF), vm((2 * ffp, wide), BF), vm((ffp, wide), BF),
            vm((cap, ffp), F32), vm((cap, ffp), F32), vm((cap, 2 * ffp), BF), vm((ffp, cap), BF), vm((ffp, cap), BF),
            vm((cap, win), F32), vm((3, cap, win), BF),
            vm((2, cap // 2, win), BF), vm((2, cap, win), BF), vm((cap, win), BF),
            vm((rows, win), BF), vm((rows, win), BF), vm((win, tok), BF), vm((ff, wide), BF), vm((ff, wide), BF),
            pltpu.SemaphoreType.REGULAR, dma((5,)), dma((6,)), dma((2,)), dma((n_c, 2)), dma((n_c, 9)), dma((n_c, 9)),
            dma((n_p, 6)), dma((n_p, 6)), dma((n_p, 2)),
        ],
        compiler_params=pltpu.CompilerParams(
            collective_id=0, has_side_effects=True, vmem_limit_bytes=VM << 20
        ),
    )(ids, probs, tok_t, cot_t, up_t, down)


def per_device(tokens, cotangent, up_weight, down_weight, expert_ids, gate_probs):
    tok, width = tokens.shape
    ff = up_weight.shape[2]
    n_exp = lax.axis_size("exp")
    n_tp = lax.axis_size("tp")
    slot = 4 * tok // n_exp
    cap = 5 * tok * n_exp // (2 * n_exp)
    ffp = -(-ff // 128) * 128
    chunks, parts = CHUNKS, PARTS
    cfg = (n_exp, n_tp, slot, cap, tok, width, ff, ffp, chunks, parts)
    tg, ug, dg = layer(
        cfg, expert_ids.T, gate_probs.T, tokens.T, cotangent.T, up_weight[0].T, down_weight[0]
    )
    return (tg.T, ug.T[None], dg[None])


def solution(mesh):
    placed = (
        P("exp", "tp"),
        P("exp", "tp"),
        P("exp", None, "tp"),
        P("exp", "tp", None),
        P("exp", None),
        P("exp", None),
    )
    return jax.shard_map(
        per_device,
        mesh=mesh,
        in_specs=placed,
        out_specs=(P("exp", "tp"), P("exp", None, "tp"), P("exp", "tp", None)),
        check_vma=False,
    )
```

```python
import functools

import jax
import jax.numpy as jnp
from jax import lax
from jax.experimental import pallas as pl
from jax.experimental.pallas import tpu as pltpu
from jax.sharding import PartitionSpec as P

BF = jnp.bfloat16
F32 = jnp.float32
MESH = pl.DeviceIdType.MESH
FAR = 1e6
AHEAD = 2
VM = 60
CHUNKS = tuple((128 * i, 128) for i in range(7))
PARTS = ((384, 128), (0, 128), (128, 128), (256, 128))


def dot(a, b, dims):
    return lax.dot_general(a, b, (dims, ((), ())), preferred_element_type=F32)


def iota(shape, dim):
    return lax.broadcasted_iota(jnp.int32, shape, dim).astype(F32)


def kernel(
    cfg,
    ids_ref, prob_ref, tok_ref, cot_ref, up_ref, down_ref,
    tg_ref, ug_ref, dg_ref,
    src, rk, ws, cnt, pick, pickw, send, recv, msend, mrecv, place, prow, pack, unpack,
    gath, wup, wdn, hid, dac, dh, dht, actt, own, pair, half, side, fin,
    rsend, rrecv, tgs, ugs, dgs,
    enter_sem, load_sem, swap_sem, meta_sem, a2a_sem, ag_s, ag_r, rs_s, rs_r, ret_sem,
):
    n_exp, n_tp, slot, cap, tok, width, ff, ffp, chunks, parts = cfg
    n_x = 4 if n_exp % 4 == 0 else 2
    chip = 2 * width
    win = parts[0][0] + parts[0][1]
    rows = n_exp * slot
    mid = cap // 2
    ny = n_tp // 2
    me = lax.axis_index("exp")
    tp = lax.axis_index("tp")
    y = tp // 2
    core = tp % 2
    sib = tp + 1 - 2 * core
    y_right, y_left, y_opp = (y + 1) % ny, (y + ny - 1) % ny, (y + 2) % ny
    right, left = 2 * y_right + core, 2 * y_left + core

    def lanes(start, size):
        return pl.ds(pl.multiple_of(start, 128), size)

    def remote(a, b, s, r, device):
        return pltpu.make_async_remote_copy(
            src_ref=a, dst_ref=b, send_sem=s, recv_sem=r, device_id=device, device_id_type=MESH
        )

    def peers(fn):
        def step(d, carry):
            fn((me + d) % n_exp)
            return carry

        lax.fori_loop(1, n_exp, step, 0)

    load_up = pltpu.make_async_copy(up_ref, wup.at[pl.ds(0, ff), :], load_sem.at[0])
    load_dn = pltpu.make_async_copy(down_ref, wdn.at[pl.ds(0, ff), :], load_sem.at[1])
    load_tok = pltpu.make_async_copy(tok_ref, src.at[pl.ds(0, width), :], load_sem.at[2])
    load_cot = pltpu.make_async_copy(cot_ref, src.at[pl.ds(width, width), :], load_sem.at[2])

    barrier = pltpu.get_barrier_semaphore()

    def signal(sem, exp, other):
        pl.semaphore_signal(sem, inc=1, device_id=(exp, other), device_id_type=MESH)

    row = [me - me % n_x + (me + d) % n_x for d in range(1, n_x)]
    column = [(me + n_x * d) % n_exp for d in range(1, n_exp // n_x)]
    for d in row + column:
        signal(barrier, d, tp)
    for other in (sib, left, right):
        signal(barrier, me, other)

    @pl.when(core == 0)
    def _():
        load_tok.start()

    @pl.when(core == 1)
    def _():
        load_cot.start()

    load_up.start()
    load_dn.start()
    swap_up = remote(
        up_ref, wup.at[pl.ds(ffp, ff), :], swap_sem.at[2], swap_sem.at[3], (me, sib)
    )

    expert = lax.broadcasted_iota(jnp.int32, (n_exp, tok), 0)
    hot0 = expert == ids_ref[0:1, :]
    hot1 = expert == ids_ref[1:2, :]
    probs = prob_ref[...].astype(F32)
    weight = jnp.where(hot0, probs[0:1, :], 0.0) + jnp.where(hot1, probs[1:2, :], 0.0)
    named = jnp.where(hot0, 1.0, 0.0) + jnp.where(hot1, 1.0, 0.0)
    earlier = jnp.where(
        lax.broadcasted_iota(jnp.int32, (tok, tok), 0)
        < lax.broadcasted_iota(jnp.int32, (tok, tok), 1),
        1.0,
        0.0,
    ).astype(BF)
    rank = dot(named.astype(BF), earlier, ((1,), (0,)))
    rk[...] = jnp.where(named > 0.0, rank, -1.0)
    ws[...] = jnp.where(core == 0, named, weight)
    cnt[...] = dot(named.astype(BF), jnp.ones((tok, 128), BF), ((1,), (0,)))

    def count_tile(e, carry):
        msend[e] = jnp.broadcast_to(cnt[pl.ds(e, 1), :], (8, 128))
        return carry

    lax.fori_loop(0, n_exp, count_tile, 0)
    mrecv[me] = msend[me]

    pl.semaphore_wait(barrier, len(row) + len(column) + 3)
    for d in row:
        signal(enter_sem, d, tp)

    swap_cot = remote(
        cot_ref, src.at[pl.ds(0, width), :], swap_sem.at[0], swap_sem.at[1], (me, sib)
    )
    swap_tok = remote(
        tok_ref, src.at[pl.ds(width, width), :], swap_sem.at[0], swap_sem.at[1], (me, sib)
    )

    @pl.when(core == 0)
    def _():
        swap_cot.start()

    @pl.when(core == 1)
    def _():
        swap_tok.start()

    swap_up.start()

    def build_pick(e, carry):
        at = pl.ds(pl.multiple_of(e * slot, slot), slot)
        hit = jnp.broadcast_to(rk[pl.ds(e, 1), :], (slot, tok)) == iota((slot, tok), 0)
        pick[at, :] = jnp.where(hit, 1.0, 0.0).astype(BF)
        pickw[at, :] = jnp.where(
            hit, jnp.broadcast_to(ws[pl.ds(e, 1), :], (slot, tok)), 0.0
        ).astype(BF)
        return carry

    lax.fori_loop(0, n_exp, build_pick, 0)

    def first(c, plane):
        start, size = chunks[c]
        return pl.multiple_of(start + plane * (chip - size - 2 * start), 128)

    def exchange(buf_from, buf_to, sems, c, c0, cw):
        mine = pl.ds(pl.multiple_of(me * slot, slot), slot)
        peers(
            lambda d: remote(
                buf_from.at[pl.ds(pl.multiple_of(d * slot, slot), slot), pl.ds(c0, cw)],
                buf_to.at[mine, pl.ds(c0, cw)],
                sems.at[c, 0],
                sems.at[c, 1],
                (d, tp),
            ).start()
        )
        buf_to[mine, pl.ds(c0, cw)] = buf_from[mine, pl.ds(c0, cw)]

    def exchanged(buf, sems, c, c0, cw, which):
        whole = buf.at[pl.ds(0, (n_exp - 1) * slot), pl.ds(c0, cw)]
        pltpu.make_async_copy(whole, whole, sems.at[c, which]).wait()

    load_tok.wait()
    block = min(rows, 256)
    def send_chunk(c):
        c0, cw = first(c, core), chunks[c][1]

        def gather_rows(i, carry):
            at = pl.ds(pl.multiple_of(i * block, block), block)
            send[at, pl.ds(c0, cw)] = dot(
                pickw[at, :], src[pl.ds(c0, cw), :], ((1,), (1,))
            ).astype(BF)
            return carry

        lax.fori_loop(0, rows // block, gather_rows, 0)

    def start_chunk(c):
        exchange(send, recv, a2a_sem, c, first(c, core), chunks[c][1])

    send_chunk(0)
    pl.semaphore_wait(enter_sem, len(row))
    peers(
        lambda d: remote(
            msend.at[d], mrecv.at[me], meta_sem.at[0], meta_sem.at[1], (d, tp)
        ).start()
    )
    start_chunk(0)
    swap_cot.wait_recv()
    for c in range(1, min(AHEAD, len(chunks))):
        send_chunk(c)
        start_chunk(c)

    wait_meta = mrecv.at[pl.ds(0, n_exp - 1)]
    pltpu.make_async_copy(wait_meta, wait_meta, meta_sem.at[1]).wait()

    def place_rows(g, before):
        at = pl.ds(pl.multiple_of(g * slot, slot), slot)
        number = iota((slot, 128), 0)
        count = mrecv[g]
        place[at, :] = jnp.where(
            number < jnp.broadcast_to(count[0:1, :], (slot, 128)),
            jnp.broadcast_to(before[0:1, :], (slot, 128)) + number,
            FAR,
        )
        return before + count

    lax.fori_loop(0, n_exp, place_rows, jnp.zeros((8, 128), F32))
    prow[...] = jnp.transpose(place[...])[0:8, :]

    def build_pack(i, carry):
        at = pl.ds(pl.multiple_of(i * 64, 64), 64)
        row = jnp.broadcast_to(prow[0:1, :], (64, rows))
        pack[at, :] = jnp.where(
            row == iota((64, rows), 0) + (i * 64).astype(F32), 1.0, 0.0
        ).astype(BF)
        return carry

    lax.fori_loop(0, cap // 64, build_pack, 0)
    for at in (ff, ffp + ff):
        wup[pl.ds(at, ffp - ff), :] = jnp.zeros((ffp - ff, ny * chip), BF)
    wdn[pl.ds(ff, ffp - ff), :] = jnp.zeros((ffp - ff, ny * chip), BF)

    def cols(yy, c, plane):
        return lanes(yy * chip + first(c, plane), chunks[c][1])

    top, low, full = pl.ds(0, mid), pl.ds(mid, mid), pl.ds(0, cap)

    def ag(k, c, receive):
        if k == 0:
            where, span, device = (y_left if receive else y), full, right
        elif k == 1:
            where, span, device = (y_right if receive else y), full, left
        elif k == 2:
            where, span, device = y, full, sib
        elif k == 3:
            where, span, device = y_left, full, sib
        elif k == 4:
            where, span, device = y_right, full, sib
        elif k == 5:
            where, span, device = (y_opp if receive else y_left), top, right
        elif k == 6:
            where, span, device = (y_opp if receive else y_right), low, left
        elif k == 7:
            where, span, device = y_opp, top, sib
        else:
            where, span, device = y_opp, low, sib
        plane = (1 - core) if (receive and k in (2, 3, 4, 7, 8)) else core
        at = gath.at[plane, span, cols(where, c, plane)]
        return remote(at, at, ag_s.at[c, k], ag_r.at[c, k], (me, device))

    def forward_near(c):
        ag(0, c, True).wait_recv()
        ag(5, c, False).start()
        ag(3, c, False).start()
        ag(1, c, True).wait_recv()
        ag(6, c, False).start()
        ag(4, c, False).start()

    def forward_far(c):
        ag(5, c, True).wait_recv()
        ag(7, c, False).start()
        ag(6, c, True).wait_recv()
        ag(8, c, False).start()

    def build_unpack(g, carry):
        at = pl.ds(pl.multiple_of(g * slot, slot), slot)
        for b in range(cap // 128):
            unpack[at, 128 * b : 128 * b + 128] = jnp.where(
                place[at, :] == iota((slot, 128), 1) + 128.0 * b, 1.0, 0.0
            ).astype(BF)
        return carry

    last = len(chunks) - 1
    for c, (c0, cw) in enumerate(chunks):
        if c + AHEAD < len(chunks):
            exchanged(send, a2a_sem, c, c0, cw, 0)
            send_chunk(c + AHEAD)
            start_chunk(c + AHEAD)
        exchanged(recv, a2a_sem, c, c0, cw, 1)
        gath[core, :, cols(y, c, core)] = dot(
            pack[...], recv[:, pl.ds(first(c, core), cw)], ((1,), (0,))
        ).astype(BF)
        for k in (0, 1, 2):
            ag(k, c, False).start()
        if c >= 1:
            forward_near(c - 1)
        if c >= 2:
            forward_far(c - 2)
        if c == 2:
            lax.fori_loop(0, n_exp, build_unpack, 0)

    load_up.wait()
    load_dn.wait()
    hid[...] = jnp.zeros_like(hid)
    dac[...] = jnp.zeros_like(dac)

    def accumulate(yy):
        at = lanes(yy * chip, chip)
        hid[...] += dot(gath[0, :, at], wup[pl.ds(0, ffp), at], ((1,), (1,)))
        dac[...] += dot(gath[1, :, at], wdn[:, at], ((1,), (1,)))

    def arrived(*kinds):
        for c in range(len(chunks)):
            for k in kinds:
                ag(k, c, True).wait_recv()

    forward_near(last)
    if last >= 1:
        forward_far(last - 1)
    arrived(2)
    accumulate(y)
    forward_far(last)

    arrived(3)
    accumulate(y_left)
    arrived(4)
    accumulate(y_right)
    arrived(7, 8)
    accumulate(y_opp)

    rb = 64

    def activate(i, carry):
        at = pl.ds(pl.multiple_of(i * rb, rb), rb)
        h = hid[at, :]
        s = jax.nn.sigmoid(h)
        dac[at, :] = dac[at, :] * (s * (1.0 + h * (1.0 - s)))
        hid[at, :] = h * s
        dh[at, 0:ffp] = dac[at, :].astype(BF)
        return carry

    lax.fori_loop(0, cap // rb, activate, 0)

    dests = (y_opp, y_right, y_left, y)
    my_win = win * core
    swap_dh = remote(
        dh.at[:, pl.ds(0, ffp)], dh.at[:, pl.ds(ffp, ffp)], swap_sem.at[4], swap_sem.at[5], (me, sib)
    )
    swap_dh.start()
    swap_up.wait_recv()
    swap_dh.wait_recv()

    base = parts[0][0]

    def only(h, fn):
        if h == 0:
            pl.when(core == 0)(fn)
        else:
            fn()

    def term(k, start, size):
        at = lanes(dests[k] * chip + start, size)
        return dot(dh[...], wup[:, at], ((1,), (0,)))

    ahead, behind = (top, low), (low, top)

    def step(h, kind, k):
        p0, pw = parts[h]
        at = pl.ds(p0, pw)
        span = behind[k] if kind == 1 else ahead[k]
        a = pair.at[0 if kind == 0 else 1 + k, span, at]
        b = half.at[k, :, at] if kind == 0 else side.at[k, span, at]
        n = 2 * kind + k
        return remote(a, b, rs_s.at[h, n], rs_r.at[h, n], (me, (right, left)[k]))

    def relay(h):
        p0, pw = parts[h]
        for k in range(2):
            step(h, 0, k).wait_recv()
            span = ahead[k]
            pair[1 + k, span, p0 : p0 + pw] = (
                pair[1 + k, span, p0 : p0 + pw].astype(F32) + half[k, :, p0 : p0 + pw].astype(F32)
            ).astype(BF)
            step(h, 2, k).start()

    def finish(h):
        p0, pw = parts[h]
        for kind in (1, 2):
            for k in range(2):
                step(h, kind, k).wait_recv()
        fin[:, p0 : p0 + pw] = (
            own[:, p0 : p0 + pw] + side[0, :, p0 : p0 + pw].astype(F32) + side[1, :, p0 : p0 + pw].astype(F32)
        ).astype(BF)
        rsend[:, p0 : p0 + pw] = dot(unpack[...], fin[:, p0 : p0 + pw], ((1,), (0,))).astype(BF)
        exchange(rsend, rrecv, ret_sem, h, p0, pw)

    gb = 512 if (ny * chip) % 512 == 0 else 128
    n_g = ny * chip // gb

    def grad_up(i, carry):
        at = lanes(i * gb, gb)
        ugs[:, at] = dot(dht[...], gath[0, :, at], ((1,), (0,)))[:ff].astype(BF)
        return carry

    def grad_down(i, carry):
        at = lanes(i * gb, gb)
        dgs[:, at] = dot(actt[...], gath[1, :, at], ((1,), (0,)))[:ff].astype(BF)
        return carry

    store_up = pltpu.make_async_copy(ugs, ug_ref, load_sem.at[3])
    store_dn = pltpu.make_async_copy(dgs, dg_ref, load_sem.at[4])
    n_h = len(parts)
    @pl.when(core == 0)
    def _():
        for k in range(3):
            pair[k, :, base:win] = term(k, base, win - base).astype(BF)
            if k == 0:
                step(0, 0, 0).start()
                step(0, 0, 1).start()
            else:
                step(0, 1, k - 1).start()
        own[:, base:win] = term(3, base, win - base)

    for k in range(3):
        pair[k, :, 0:base] = term(k, my_win, base).astype(BF)
        if k == 0:
            step(1, 0, 0).start()
            step(1, 0, 1).start()
        else:
            step(1, 1, k - 1).start()
    for k in range(2):
        step(2, 0, k).start()
    own[:, 0:base] = term(3, my_win, base)
    dht[...] = jnp.transpose(dac[...]).astype(BF)
    for h in range(n_h):
        only(h, functools.partial(relay, h))
        if h > 0:
            for kind, q in ((1, h + 1), (0, h + 2)):
                if q < n_h:
                    for k in range(2):
                        step(q, kind, k).start()
            only(h - 1, functools.partial(finish, h - 1))
        lax.fori_loop(h * n_g // n_h, (h + 1) * n_g // n_h, grad_up, 0)
    store_up.start()
    finish(n_h - 1)
    actt[...] = jnp.transpose(hid[...]).astype(BF)
    lax.fori_loop(0, ny * chip // gb, grad_down, 0)
    store_dn.start()

    shift = width - base
    swap_tg = remote(
        tgs.at[pl.ds(width, win - width), :], tgs.at[pl.ds(0, shift), :],
        swap_sem.at[6], swap_sem.at[7], (me, sib),
    )

    def combine(h):
        p0, pw = parts[h]
        exchanged(rrecv, ret_sem, h, p0, pw, 1)
        at = pl.ds(pl.multiple_of(p0 + shift * core, 64), pw)
        tgs[at, :] = dot(rrecv[:, p0 : p0 + pw], pick[...], ((0,), (0,))).astype(BF)

    @pl.when(core == 0)
    def _():
        combine(0)
        swap_tg.start()

    for h in range(1, n_h):
        combine(h)

    @pl.when(core == 1)
    def _():
        swap_tg.wait_recv()

    result = pltpu.make_async_copy(tgs.at[pl.ds(0, width), :], tg_ref, load_sem.at[2])
    result.start()

    swap_cot.wait_send()
    wait_meta = msend.at[pl.ds(0, n_exp - 1)]
    pltpu.make_async_copy(wait_meta, wait_meta, meta_sem.at[0]).wait()
    for c, (c0, cw) in enumerate(chunks):
        if c + AHEAD >= len(chunks):
            exchanged(send, a2a_sem, c, c0, cw, 0)
        for k in range(9):
            ag(k, c, False).wait_send()
    swap_up.wait_send()
    swap_dh.wait_send()
    def sent(h):
        p0, pw = parts[h]
        for kind in range(3):
            for k in range(2):
                step(h, kind, k).wait_send()
        exchanged(rsend, ret_sem, h, p0, pw, 0)
        if h == 0:
            swap_tg.wait_send()

    for h in range(n_h):
        only(h, functools.partial(sent, h))
    store_up.wait()
    store_dn.wait()
    result.wait()


def layer(cfg, ids, probs, tok_t, cot_t, up_t, down):
    n_exp, n_tp, slot, cap, tok, width, ff, ffp, chunks, parts = cfg
    chip = 2 * width
    wide = n_tp * width
    rows = n_exp * slot
    win = parts[0][0] + parts[0][1]
    n_c, n_p = len(chunks), len(parts)
    vm = pltpu.VMEM
    dma = pltpu.SemaphoreType.DMA
    hbm = pl.BlockSpec(memory_space=pl.ANY)
    vmem = pl.BlockSpec(memory_space=pltpu.VMEM)
    return pl.pallas_call(
        functools.partial(kernel, cfg),
        out_shape=(
            jax.ShapeDtypeStruct((width, tok), BF),
            jax.ShapeDtypeStruct((ff, wide), BF),
            jax.ShapeDtypeStruct((ff, wide), BF),
        ),
        in_specs=[vmem, vmem] + [pl.BlockSpec(memory_space=pltpu.HBM)] * 4,
        out_specs=(hbm, hbm, hbm),
        scratch_shapes=[
            vm((chip, tok), BF), vm((n_exp, tok), F32), vm((n_exp, tok), F32), vm((n_exp, 128), F32),
            vm((rows, tok), BF), vm((rows, tok), BF), vm((rows, chip), BF), vm((rows, chip), BF),
            vm((n_exp, 8, 128), F32), vm((n_exp, 8, 128), F32), vm((rows, 128), F32), vm((8, rows), F32),
            vm((cap, rows), BF), vm((rows, cap), BF),
            vm((2, cap, wide), BF), vm((2 * ffp, wide), BF), vm((ffp, wide), BF),
            vm((cap, ffp), F32), vm((cap, ffp), F32), vm((cap, 2 * ffp), BF), vm((ffp, cap), BF), vm((ffp, cap), BF),
            vm((cap, win), F32), vm((3, cap, win), BF),
            vm((2, cap // 2, win), BF), vm((2, cap, win), BF), vm((cap, win), BF),
            vm((rows, win), BF), vm((rows, win), BF), vm((win, tok), BF), vm((ff, wide), BF), vm((ff, wide), BF),
            pltpu.SemaphoreType.REGULAR, dma((5,)), dma((8,)), dma((2,)), dma((n_c, 2)), dma((n_c, 9)), dma((n_c, 9)),
            dma((n_p, 6)), dma((n_p, 6)), dma((n_p, 2)),
        ],
        compiler_params=pltpu.CompilerParams(
            collective_id=0, has_side_effects=True, vmem_limit_bytes=VM << 20
        ),
    )(ids, probs, tok_t, cot_t, up_t, down)


def per_device(tokens, cotangent, up_weight, down_weight, expert_ids, gate_probs):
    tok, width = tokens.shape
    ff = up_weight.shape[2]
    n_exp = lax.axis_size("exp")
    n_tp = lax.axis_size("tp")
    slot = 4 * tok // n_exp
    cap = 5 * tok * n_exp // (2 * n_exp)
    ffp = -(-ff // 128) * 128
    chunks, parts = CHUNKS, PARTS
    cfg = (n_exp, n_tp, slot, cap, tok, width, ff, ffp, chunks, parts)
    tg, ug, dg = layer(
        cfg, expert_ids.T, gate_probs.T, tokens.T, cotangent.T, up_weight[0].T, down_weight[0]
    )
    return (tg.T, ug.T[None], dg[None])


def solution(mesh):
    placed = (
        P("exp", "tp"),
        P("exp", "tp"),
        P("exp", None, "tp"),
        P("exp", "tp", None),
        P("exp", None),
        P("exp", None),
    )
    return jax.shard_map(
        per_device,
        mesh=mesh,
        in_specs=placed,
        out_specs=(P("exp", "tp"), P("exp", None, "tp"), P("exp", "tp", None)),
        check_vma=False,
    )
```
